32 devices in a mesh: leaf: 2 (over y), user: 4 (over x, core), tensor: 4 (over z).
Axes of the slice: x: 2, y: 2, z: 4, core: 2. Of those that a mesh axis runs over, the one named last changes fastest.
Arguments:
- user_feat: bfloat16 [32, 128], P('user'), may hold values from -6 to 6
- beam_nodes: int32 [32, 128], P('user', ('leaf', 'tensor')), may hold values from 0 to 16383, as said below
- item_ids: int32 [32, 384], P('user', 'leaf'), may hold values from 0 to 16383, as said below
- subtree_slot: int32 [32], replicated, may hold values from 0 to 31, as said below
- node_table: bfloat16 [16384, 128], P(('leaf', 'tensor')), may hold values from -6 to 6
- item_table: bfloat16 [16384, 128], P(('leaf', 'tensor')), may hold values from -6 to 6
- mlp_user: bfloat16 [128, 1024], replicated, may hold values from -0.375 to 0.375
- mlp_node: bfloat16 [128, 1024], replicated, may hold values from -0.375 to 0.375
- mlp_bias: float32 [1024], replicated, may hold values from -3 to 3
- mlp_out: bfloat16 [1024], replicated, may hold values from -0.1875 to 0.1875
- proj_in: bfloat16 [384, 2048], P(None, 'tensor'), may hold values from -0.3125 to 0.3125
- cross_w: bfloat16 [2, 2048, 2048], P(None, None, 'tensor'), may hold values from -0.125 to 0.125
- cross_b: float32 [2, 2048], P(None, 'tensor'), may hold values from -3 to 3
- out_w: bfloat16 [2048], P('tensor'), may hold values from -0.125 to 0.125
Outputs:
- beam_score: float32 [32, 128], P('user', ('leaf', 'tensor'))
- interest: float32 [32, 128], P('user')
- logit: float32 [32, 384], P('user', 'leaf')
The draws below stay inside these ranges and needn't reach their ends.
Inputs may be any that keep to these rules, and one draw needn't show every extreme that they name: A permutation of the subtrees: subtree s is held by index subtree_slot[s] // 4 of leaf+tensor (leaf-major), as its block subtree_slot[s] % 4. `beam_nodes`: within the 8 x 16 block of one device, at most 16 nodes belong to subtrees held by any one index of leaf+tensor; some index receives exactly 16 from every device's block. `item_ids`: split a device's 8 x 192 block, flattened user by user, into 4 runs of 384 items; each run has at most 48 items of subtrees held by any one index of leaf+tensor, and some index receives exactly 48 from every run.
All inputs are finite; a program needn't handle non-finite values.
Results may differ from the reference program's by a relative error of at most 0.0062.
Values may be sent and summed in bfloat16 or wider, within the bound.
A program may use at most 64 MiB of HBM per device.

```python
import math
import jax
import jax.numpy as jnp
from jax import lax

E = 128
H = 1024
W = 2048
LAYERS = 2
SUB_NODES = 512
SUB_ITEMS = 512
SUB_DEV = 4
U_DEV = 8
BEAM_DEV = 16
ITEM_DEV = 192
USERS = 32
BEAM = 128
K = 384
NODES = 16384
ITEMS = 16384
CAP_B = 16
FETCH = 384
CAP_I = 48
N_LEAF = 2
N_USER = 4
N_TENSOR = 4


def slot_table(key):
    return jax.random.permutation(jax.random.fold_in(key, 7), SUB_DEV * N_LEAF * N_TENSOR).astype(jnp.int32)


def owner_blocks(key, blocks, per_block, owners, capacity):
    hot = jax.random.randint(jax.random.fold_in(key, 11), (), 0, owners)
    keys = jax.random.split(jax.random.fold_in(key, 12), blocks)

    def one_block(block_key):
        order_key, shuffle_key = jax.random.split(block_key)
        others = jax.random.permutation(order_key, owners - 1).astype(jnp.int32)
        place = jnp.arange(per_block, dtype=jnp.int32)
        spread = others[jnp.maximum(place - capacity, 0) % (owners - 1)]
        owner = jnp.where(place < capacity, hot, (hot + 1 + spread) % owners)
        return jax.random.permutation(shuffle_key, owner.astype(jnp.int32))
    return jax.vmap(one_block)(keys)


def ids_from_owners(key, salt, owner, span):
    slot_map = slot_table(key)
    subtree_of = jnp.argsort(slot_map).astype(jnp.int32)
    pick = jax.random.randint(jax.random.fold_in(key, salt + 1), owner.shape, 0, SUB_DEV)
    within = jax.random.randint(jax.random.fold_in(key, salt + 2), owner.shape, 0, span)
    subtree = subtree_of[owner * SUB_DEV + pick]
    return (subtree * span + within).astype(jnp.int32)


def draw_subtree_slot(key, part):
    return slot_table(key)


def draw_beam_nodes(key, part):
    owners = N_LEAF * N_TENSOR
    owner = owner_blocks(jax.random.fold_in(key, 100), N_USER * owners, U_DEV * BEAM_DEV, owners, CAP_B)
    ids = ids_from_owners(key, 100, owner, SUB_NODES)
    ids = ids.reshape(N_USER, owners, U_DEV, BEAM_DEV).transpose(0, 2, 1, 3)
    return ids.reshape(USERS, BEAM)


def draw_item_ids(key, part):
    owners = N_LEAF * N_TENSOR
    owner = owner_blocks(jax.random.fold_in(key, 200), N_USER * N_LEAF * N_TENSOR, FETCH, owners, CAP_I)
    ids = ids_from_owners(key, 200, owner, SUB_ITEMS)
    ids = ids.reshape(N_USER, N_LEAF, U_DEV, ITEM_DEV).transpose(0, 2, 1, 3)
    return ids.reshape(USERS, K)


def block_scale(key, extent, cuts, low, top_value):
    level = 1.0
    for axis_at, parts in cuts:
        steps = jax.random.uniform(jax.random.fold_in(jax.random.fold_in(key, 6), axis_at), (parts,), jnp.float32, low / len(cuts), top_value / len(cuts))
        level = level * jnp.repeat(jnp.exp(steps), extent[axis_at] // parts).reshape((-1,) + (1,) * (len(extent) - 1 - axis_at))
    return level


def gaussian(own_key, extent, width, limit, cuts=(), kind=jnp.bfloat16):
    values = width * jax.random.normal(own_key, extent, jnp.float32)
    if cuts:
        values = values * block_scale(own_key, extent, cuts, -0.22, 0.18)
    return jnp.clip(values, -limit, limit).astype(kind)


def setup_inputs(seed: int = 0) -> dict:
    arg_keys = jax.random.split(jax.random.key(seed), 15)
    return {
        "user_feat": gaussian(arg_keys[0], (USERS, E), 1.0, 6.0, ((0, 4),)),
        "beam_nodes": draw_beam_nodes(jax.random.fold_in(arg_keys[14], 71), 0),
        "item_ids": draw_item_ids(jax.random.fold_in(arg_keys[14], 71), 0),
        "subtree_slot": draw_subtree_slot(jax.random.fold_in(arg_keys[14], 71), 0),
        "node_table": gaussian(arg_keys[4], (NODES, E), 1.0, 6.0, ((0, 8),)),
        "item_table": gaussian(arg_keys[5], (ITEMS, E), 1.0, 6.0, ((0, 8),)),
        "mlp_user": gaussian(arg_keys[6], (E, H), (2 * E) ** -0.5, 0.375),
        "mlp_node": gaussian(arg_keys[7], (E, H), (2 * E) ** -0.5, 0.375),
        "mlp_bias": gaussian(arg_keys[8], (H,), 0.5, 3.0, (), jnp.float32),
        "mlp_out": gaussian(arg_keys[9], (H,), H ** -0.5, 0.1875),
        "proj_in": gaussian(arg_keys[10], (3 * E, W), (3 * E) ** -0.5, 0.3125, ((1, 4),)),
        "cross_w": gaussian(arg_keys[11], (LAYERS, W, W), W ** -0.5, 0.125, ((2, 4),)),
        "cross_b": gaussian(arg_keys[12], (LAYERS, W), 0.5, 3.0, ((1, 4),), jnp.float32),
        "out_w": gaussian(arg_keys[13], (W,), W ** -0.5, 0.125, ((0, 4),)),
    }


def reference(user_feat, beam_nodes, item_ids, subtree_slot, node_table, item_table, mlp_user, mlp_node, mlp_bias, mlp_out, proj_in, cross_w, cross_b, out_w):
    node_row = subtree_slot[beam_nodes // SUB_NODES] * SUB_NODES + beam_nodes % SUB_NODES
    node_vec = node_table[node_row]
    user_part = jnp.dot(user_feat, mlp_user, preferred_element_type=jnp.float32)
    node_part = jnp.dot(node_vec.reshape(USERS * BEAM, E), mlp_node, preferred_element_type=jnp.float32).reshape(USERS, BEAM, H)
    hidden = jax.nn.silu(user_part[:, None, :] + node_part + mlp_bias).astype(jnp.bfloat16)
    beam_score = jnp.dot(hidden.reshape(USERS * BEAM, H), mlp_out, preferred_element_type=jnp.float32).reshape(USERS, BEAM)
    weights = jax.nn.sigmoid(beam_score)
    interest = jnp.einsum('ub,ube->ue', weights, node_vec.astype(jnp.float32), precision=lax.Precision.HIGHEST) / math.sqrt(BEAM)
    item_row = subtree_slot[item_ids // SUB_ITEMS] * SUB_ITEMS + item_ids % SUB_ITEMS
    item_vec = item_table[item_row]
    interest_b = interest.astype(jnp.bfloat16)
    user_cols = jnp.broadcast_to(user_feat[:, None, :], (USERS, K, E))
    interest_cols = jnp.broadcast_to(interest_b[:, None, :], (USERS, K, E))
    inputs = jnp.concatenate([user_cols, interest_cols, item_vec], axis=2).reshape(USERS * K, 3 * E)
    x_first = jnp.dot(inputs, proj_in, preferred_element_type=jnp.float32).astype(jnp.bfloat16)
    x_now = x_first
    for layer in range(LAYERS):
        mixed = jnp.dot(x_now, cross_w[layer], preferred_element_type=jnp.float32) + cross_b[layer]
        x_now = (x_first.astype(jnp.float32) * mixed + x_now.astype(jnp.float32)).astype(jnp.bfloat16)
    logit = jnp.dot(x_now, out_w, preferred_element_type=jnp.float32).reshape(USERS, K)
    return (beam_score, interest, logit)
```

```python
import math

import jax
import jax.numpy as jnp
from jax import lax
from jax.sharding import PartitionSpec as P

SUB_NODES = 512
SUB_ITEMS = 512
BOTH = ("leaf", "tensor")
F32 = jnp.float32
BF16 = jnp.bfloat16


def small_lookup(table, index):
    hits = index[..., None] == jnp.arange(table.shape[0], dtype=jnp.int32)
    return jnp.sum(jnp.where(hits, table, 0), axis=-1)


def locate(ids, span, subtree_slot, rows):
    slot = small_lookup(subtree_slot, ids // span)
    per = rows // span
    return slot // per, slot % per * span + ids % span


def rank_in_row(marks):
    n = marks.shape[-1]
    at = jnp.arange(n, dtype=jnp.int32)
    before = (at[:, None] < at[None, :]).astype(BF16)
    return jnp.dot(marks.astype(BF16), before, preferred_element_type=F32).astype(jnp.int32)


def pick_rows(table, wanted):
    hot = (wanted[:, None] == jnp.arange(table.shape[0], dtype=jnp.int32)[None, :]).astype(BF16)
    return jnp.dot(hot, table, preferred_element_type=F32).astype(BF16)


def owned_slots(owner, local, me, cap):
    mine = owner == me
    rank = rank_in_row(mine)
    chosen = mine[:, None, :] & (
        rank[:, None, :] == jnp.arange(cap, dtype=jnp.int32)[None, :, None]
    )
    wanted = jnp.sum(jnp.where(chosen, local[:, None, :] + 1, 0), axis=2) - 1
    return chosen, wanted


def per_device(
    user_feat,
    beam_nodes,
    item_ids,
    subtree_slot,
    node_table,
    item_table,
    mlp_user,
    mlp_node,
    mlp_bias,
    mlp_out,
    proj_in,
    cross_w,
    cross_b,
    out_w,
):
    leafs = lax.axis_size("leaf")
    tensors = lax.axis_size("tensor")
    owners = leafs * tensors
    tensor_at = lax.axis_index("tensor")
    me = lax.axis_index("leaf") * tensors + tensor_at
    users, beam = beam_nodes.shape
    items = item_ids.shape[1]
    width = user_feat.shape[1]

    proj_all = lax.all_gather(proj_in, "tensor", axis=1, tiled=True)
    first_here = jnp.dot(proj_all, cross_w[0], preferred_element_type=F32).astype(BF16)
    first_all = lax.all_gather(first_here, "tensor", axis=1, tiled=True)
    bias_all = lax.all_gather(cross_b[0], "tensor", axis=0, tiled=True)

    requests = users * beam
    cap_b = max(2, -(-requests // owners))
    node_ids = lax.all_gather(beam_nodes.reshape(-1), BOTH, axis=0)
    n_owner, n_local = locate(node_ids, SUB_NODES, subtree_slot, node_table.shape[0])
    n_chosen, n_wanted = owned_slots(n_owner, n_local, me, cap_b)
    asker = jnp.arange(requests, dtype=jnp.int32) // beam
    n_user = jnp.sum(jnp.where(n_chosen, asker[None, None, :], 0), axis=2).reshape(-1)
    node_rows = pick_rows(node_table, n_wanted.reshape(-1))
    user_hot = n_user[:, None] == jnp.arange(users, dtype=jnp.int32)[None, :]
    user_rows = jnp.dot(user_hot.astype(BF16), user_feat, preferred_element_type=F32).astype(BF16)
    pre = (
        jnp.dot(user_rows, mlp_user, preferred_element_type=F32)
        + jnp.dot(node_rows, mlp_node, preferred_element_type=F32)
        + mlp_bias
    )
    hidden = jax.nn.silu(pre).astype(BF16)
    scores = jnp.dot(hidden, mlp_out, preferred_element_type=F32)
    held = n_wanted.reshape(-1) >= 0
    gate = jnp.where(user_hot & held[:, None], jax.nn.sigmoid(scores)[:, None], 0.0)
    numerator = lax.dot_general(
        gate, node_rows.astype(F32), (((0,), (0,)), ((), ())), precision=lax.Precision.HIGHEST
    )
    back = jnp.sum(jnp.where(n_chosen, scores.reshape(owners, cap_b, 1), 0.0), axis=1)
    summed = lax.psum(jnp.concatenate([numerator.reshape(-1), back.reshape(-1)]), BOTH)
    interest = summed[: users * width].reshape(users, width) / math.sqrt(owners * beam)
    beam_score = lax.dynamic_slice(
        summed, (users * width + me * requests,), (requests,)
    ).reshape(users, beam)

    rows = users * items
    fetch = rows // tensors
    cap_i = max(2, -(-fetch // owners))
    item_all = lax.all_gather(item_ids.reshape(-1), "leaf", axis=0).reshape(owners, fetch)
    i_owner, i_local = locate(item_all, SUB_ITEMS, subtree_slot, item_table.shape[0])
    _, i_wanted = owned_slots(i_owner, i_local, me, cap_i)
    sent = pick_rows(item_table, i_wanted.reshape(-1)).reshape(owners, cap_i, width)
    arrived = lax.all_to_all(sent, BOTH, split_axis=0, concat_axis=0, tiled=True)
    my_owner = lax.dynamic_slice(i_owner, (me, 0), (1, fetch))[0]
    marks = my_owner[None, :] == jnp.arange(owners, dtype=jnp.int32)[:, None]
    place = jnp.sum(jnp.where(marks, rank_in_row(marks), 0), axis=0) + my_owner * cap_i
    run_rows = pick_rows(arrived.reshape(owners * cap_i, width), place)
    item_rows = lax.all_gather(run_rows, "tensor", axis=0, tiled=True)

    shared = jnp.concatenate([user_feat, interest.astype(BF16)], axis=1)
    two = 2 * width
    base0 = jnp.dot(shared, proj_all[:two], preferred_element_type=F32)
    base1 = jnp.dot(shared, first_all[:two], preferred_element_type=F32) + bias_all
    x0 = jnp.dot(item_rows, proj_all[two:], preferred_element_type=F32).reshape(users, items, -1)
    mixed = jnp.dot(item_rows, first_all[two:], preferred_element_type=F32).reshape(users, items, -1)
    x0 = x0 + base0[:, None, :]
    mixed = mixed + base1[:, None, :]
    x1 = (x0 * mixed + x0).astype(BF16).reshape(rows, -1)
    second = jnp.dot(x1, cross_w[1], preferred_element_type=F32)
    cols = proj_in.shape[1]
    x0_here = lax.dynamic_slice(x0.astype(BF16).reshape(rows, -1), (0, tensor_at * cols), (rows, cols))
    x1_here = lax.dynamic_slice(x1, (0, tensor_at * cols), (rows, cols))
    x2 = x0_here.astype(F32) * (second + cross_b[1]) + x1_here.astype(F32)
    partial = jnp.sum(x2 * out_w.astype(F32), axis=1)
    logit = lax.psum(partial, "tensor").reshape(users, items)
    return (beam_score, interest, logit)


def solution(mesh):
    placed = (
        P("user", None),
        P("user", BOTH),
        P("user", "leaf"),
        P(),
        P(BOTH, None),
        P(BOTH, None),
        P(),
        P(),
        P(),
        P(),
        P(None, "tensor"),
        P(None, None, "tensor"),
        P(None, "tensor"),
        P("tensor"),
    )
    return jax.shard_map(
        per_device,
        mesh=mesh,
        in_specs=placed,
        out_specs=(P("user", BOTH), P("user", None), P("user", "leaf")),
        check_vma=False,
    )
```

```python
import functools
import math

import jax
import jax.numpy as jnp
from jax import lax
from jax.experimental import pallas as pl
from jax.experimental.pallas import tpu as pltpu
from jax.sharding import PartitionSpec as P

SUB_NODES = 512
SUB_ITEMS = 512
BOTH = ("leaf", "tensor")
F32 = jnp.float32
BF16 = jnp.bfloat16


def small_lookup(table, index):
    hits = index[..., None] == jnp.arange(table.shape[0], dtype=jnp.int32)
    return jnp.sum(jnp.where(hits, table, 0), axis=-1)


def locate(ids, span, subtree_slot, rows):
    slot = small_lookup(subtree_slot, ids // span)
    per = rows // span
    return slot // per, slot % per * span + ids % span


def rank_in_row(marks):
    n = marks.shape[-1]
    at = jnp.arange(n, dtype=jnp.int32)
    before = (at[:, None] < at[None, :]).astype(BF16)
    return jnp.dot(marks.astype(BF16), before, preferred_element_type=F32).astype(jnp.int32)


def pick_rows(table, wanted):
    hot = (wanted[:, None] == jnp.arange(table.shape[0], dtype=jnp.int32)[None, :]).astype(BF16)
    return jnp.dot(hot, table, preferred_element_type=F32).astype(BF16)


def exchange_kernel(modes, leafs, tensors, wide, *refs):
    n = len(modes)
    srcs, outs, send_sems, recv_sems = refs[:n], refs[n : 2 * n], refs[2 * n], refs[2 * n + 1]
    leaf, tensor = lax.axis_index("leaf"), lax.axis_index("tensor")
    size = leafs * tensors if wide else tensors
    me = leaf * tensors + tensor if wide else tensor

    def target(k):
        peer = (me + k) % size
        if wide:
            return peer, peer // tensors, peer % tensors
        return peer, leaf, peer

    def part(mode, src, peer, peer_leaf):
        if mode == "peer":
            return src.at[peer]
        if mode == "leaf":
            return src.at[peer_leaf]
        return src

    def copies(k):
        peer, peer_leaf, peer_tensor = target(k)
        return [
            pltpu.make_async_remote_copy(
                src_ref=part(mode, src, peer, peer_leaf),
                dst_ref=out.at[me],
                send_sem=send_sems.at[i, k - 1],
                recv_sem=recv_sems.at[i, k - 1],
                device_id={"leaf": peer_leaf, "tensor": peer_tensor},
                device_id_type=pl.DeviceIdType.MESH,
            )
            for i, (mode, src, out) in enumerate(zip(modes, srcs, outs))
        ]

    barrier = pltpu.get_barrier_semaphore()

    @pl.loop(1, size)
    def _(k):
        _, peer_leaf, peer_tensor = target(k)
        pl.semaphore_signal(
            barrier,
            inc=1,
            device_id={"leaf": peer_leaf, "tensor": peer_tensor},
            device_id_type=pl.DeviceIdType.MESH,
        )

    pl.semaphore_wait(barrier, size - 1)

    @pl.loop(1, size)
    def _(k):
        for copy in copies(k):
            copy.start()

    for mode, src, out in zip(modes, srcs, outs):
        out[me] = part(mode, src, me, leaf)[...]

    @pl.loop(1, size)
    def _(k):
        for copy in copies(k):
            copy.wait()


def exchange(collective_id, wide, *entries):
    leafs, tensors = lax.axis_size("leaf"), lax.axis_size("tensor")
    size = leafs * tensors if wide else tensors
    modes = tuple(mode for mode, _ in entries)
    arrays = [array for _, array in entries]
    outs = [
        jax.ShapeDtypeStruct((size,) + (a.shape if mode == "all" else a.shape[1:]), a.dtype)
        for mode, a in entries
    ]
    return pl.pallas_call(
        functools.partial(exchange_kernel, modes, leafs, tensors, wide),
        out_shape=outs,
        in_specs=[pl.BlockSpec(memory_space=pltpu.VMEM)] * len(arrays),
        out_specs=[pl.BlockSpec(memory_space=pltpu.VMEM)] * len(arrays),
        scratch_shapes=[
            pltpu.SemaphoreType.DMA((len(arrays), size - 1)),
            pltpu.SemaphoreType.DMA((len(arrays), size - 1)),
        ],
        compiler_params=pltpu.CompilerParams(
            collective_id=collective_id, has_side_effects=True, vmem_limit_bytes=32 << 20
        ),
    )(*arrays)


def rank_kernel_body(
    tensors, rows_ref, proj_ref, first_ref, own_proj, own_first, base0, base1, own0, own1,
    cross, bias, weight, out_ref,
):
    rows = rows_ref[0]
    cols = own_proj.shape[1]
    dot = functools.partial(jnp.dot, preferred_element_type=F32)
    second = jnp.zeros((rows.shape[0], cols), F32)
    for t in range(tensors):
        x0 = dot(rows, proj_ref[t]) + base0[0, t : t + 1]
        mixed = dot(rows, first_ref[t]) + base1[0, t : t + 1]
        x1 = (x0 * mixed + x0).astype(BF16)
        second += dot(x1, cross[t * cols : (t + 1) * cols, :])
    x0 = dot(rows, own_proj[...]) + own0[0]
    x1 = x0 * (dot(rows, own_first[...]) + own1[0]) + x0
    x2 = x0 * (second + bias[...]) + x1
    out_ref[0] = lax.dot_general(
        weight[...], x2, (((1,), (1,)), ((), ())),
        precision=lax.Precision.HIGHEST, preferred_element_type=F32,
    )


def rank_rows(rows, proj_all, first_all, proj, first, base0, base1, own0, own1, cross, bias, weight):
    users, items, width = rows.shape
    tensors, _, cols = proj_all.shape
    full3 = pl.BlockSpec((tensors, width, cols), lambda u: (0, 0, 0))
    own = pl.BlockSpec((width, cols), lambda u: (0, 0))
    line = pl.BlockSpec((1, cols), lambda u: (0, 0))
    return pl.pallas_call(
        functools.partial(rank_kernel_body, tensors),
        grid=(users,),
        out_shape=jax.ShapeDtypeStruct((users, 1, items), F32),
        in_specs=[
            pl.BlockSpec((1, items, width), lambda u: (u, 0, 0)),
            full3, full3, own, own,
            pl.BlockSpec((1, tensors, cols), lambda u: (u, 0, 0)),
            pl.BlockSpec((1, tensors, cols), lambda u: (u, 0, 0)),
            pl.BlockSpec((1, 1, cols), lambda u: (u, 0, 0)),
            pl.BlockSpec((1, 1, cols), lambda u: (u, 0, 0)),
            pl.BlockSpec(cross.shape, lambda u: (0, 0)),
            line, line,
        ],
        out_specs=pl.BlockSpec((1, 1, items), lambda u: (u, 0, 0)),
        compiler_params=pltpu.CompilerParams(vmem_limit_bytes=40 << 20),
    )(rows, proj_all, first_all, proj, first, base0, base1, own0, own1, cross, bias, weight)


def request_lists(owner, coded, owners, cap):
    marks = owner[None, :] == jnp.arange(owners, dtype=jnp.int32)[:, None]
    rank = rank_in_row(marks)
    chosen = marks[:, None, :] & (
        rank[:, None, :] == jnp.arange(cap, dtype=jnp.int32)[None, :, None]
    )
    return chosen, jnp.sum(jnp.where(chosen, coded + 1, 0), axis=2) - 1


def per_device(
    user_feat,
    beam_nodes,
    item_ids,
    subtree_slot,
    node_table,
    item_table,
    mlp_user,
    mlp_node,
    mlp_bias,
    mlp_out,
    proj_in,
    cross_w,
    cross_b,
    out_w,
):
    leafs = lax.axis_size("leaf")
    tensors = lax.axis_size("tensor")
    owners = leafs * tensors
    tensor_at = lax.axis_index("tensor")
    users, beam = beam_nodes.shape
    items = item_ids.shape[1]
    width = user_feat.shape[1]
    two = 2 * width
    cols = proj_in.shape[1]

    proj_here = proj_in[two:]
    proj_all = lax.all_gather(proj_here, "tensor", axis=0)
    flat_proj = jnp.moveaxis(proj_all, 0, 1).reshape(width, tensors * cols)
    first_here = jnp.dot(flat_proj, cross_w[0], preferred_element_type=F32).astype(BF16)
    first_all = lax.all_gather(first_here, "tensor", axis=0)

    requests = users * beam
    cap_b = max(2, -(-requests // owners))
    n_owner, n_local = locate(beam_nodes.reshape(-1), SUB_NODES, subtree_slot, node_table.shape[0])
    asker = jnp.arange(requests, dtype=jnp.int32) // beam
    n_chosen, n_list = request_lists(n_owner, n_local * users + asker, owners, cap_b)
    rows = users * items
    fetch = rows // tensors
    cap_i = max(2, -(-fetch // owners))
    i_owner, i_local = locate(item_ids.reshape(-1), SUB_ITEMS, subtree_slot, item_table.shape[0])
    i_owner, i_local = i_owner.reshape(tensors, fetch), i_local.reshape(tensors, fetch)
    run_owner = lax.dynamic_slice(i_owner, (tensor_at, 0), (1, fetch))[0]
    run_local = lax.dynamic_slice(i_local, (tensor_at, 0), (1, fetch))[0]
    _, i_list = request_lists(run_owner, run_local, owners, cap_i)
    lists = jnp.concatenate([n_list, i_list], axis=1)
    lanes = -(-lists.shape[1] // 128) * 128
    lists = jnp.pad(lists, ((0, 0), (0, lanes - lists.shape[1])))[:, None, :]
    (asked,) = exchange(0, True, ("peer", lists))
    n_asked = asked[:, 0, :cap_b].reshape(-1)
    i_asked = asked[:, 0, cap_b : cap_b + cap_i].reshape(-1)

    sent = pick_rows(item_table, i_asked).reshape(leafs, tensors * cap_i, width)
    held = n_asked >= 0
    node_rows = pick_rows(node_table, jnp.where(held, n_asked // users, -1))
    user_hot = (n_asked % users)[:, None] == jnp.arange(users, dtype=jnp.int32)[None, :]
    user_rows = jnp.dot(user_hot.astype(BF16), user_feat, preferred_element_type=F32).astype(BF16)
    pre = (
        jnp.dot(user_rows, mlp_user, preferred_element_type=F32)
        + jnp.dot(node_rows, mlp_node, preferred_element_type=F32)
        + mlp_bias
    )
    hidden = jax.nn.silu(pre).astype(BF16)
    scores = jnp.dot(hidden, mlp_out, preferred_element_type=F32)
    gate = jnp.where(user_hot & held[:, None], jax.nn.sigmoid(scores)[:, None], 0.0)
    numerator = lax.dot_general(
        gate, node_rows.astype(F32), (((0,), (0,)), ((), ())), precision=lax.Precision.HIGHEST
    )
    back_lanes = -(-cap_b // 128) * 128
    back = jnp.pad(scores.reshape(owners, cap_b), ((0, 0), (0, back_lanes - cap_b)))[:, None, :]
    sums, scored, arrived = exchange(
        1, True, ("all", numerator), ("peer", back), ("leaf", sent)
    )
    interest = jnp.sum(sums, axis=0) / math.sqrt(owners * beam)
    own_scores = scored[:, 0, :cap_b]
    beam_score = jnp.sum(
        jnp.where(n_chosen, own_scores[:, :, None], 0.0), axis=(0, 1)
    ).reshape(users, beam)

    shared = jnp.concatenate([user_feat, interest.astype(BF16)], axis=1)
    own0 = jnp.dot(shared, proj_in[:two], preferred_element_type=F32)
    (all0,) = exchange(2, False, ("all", own0))
    base0 = jnp.moveaxis(all0, 0, 1)
    flat0 = base0.reshape(users, tensors * cols).astype(BF16)
    own1 = jnp.dot(flat0, cross_w[0], preferred_element_type=F32) + cross_b[0]
    (all1,) = exchange(3, False, ("all", own1))
    base1 = jnp.moveaxis(all1, 0, 1)

    run_marks = i_owner[:, None, :] == jnp.arange(owners, dtype=jnp.int32)[None, :, None]
    run_rank = jnp.sum(jnp.where(run_marks, rank_in_row(run_marks), 0), axis=1)
    place = run_rank + i_owner * cap_i
    by_run = jnp.moveaxis(arrived.reshape(owners, tensors, cap_i, width), 1, 0)
    hot = (place[:, :, None] == jnp.arange(owners * cap_i, dtype=jnp.int32)).astype(BF16)
    item_rows = jnp.einsum(
        "tfs,tsd->tfd", hot, by_run.reshape(tensors, owners * cap_i, width),
        preferred_element_type=F32,
    ).astype(BF16).reshape(users, items, width)

    partial = rank_rows(
        item_rows, proj_all, first_all, proj_here, first_here, base0, base1,
        own0[:, None, :], own1[:, None, :], cross_w[1], cross_b[1][None, :],
        out_w.astype(F32)[None, :],
    )
    (parts,) = exchange(4, False, ("all", partial.reshape(users, items)))
    logit = jnp.sum(parts, axis=0)
    return (beam_score, interest, logit)


def solution(mesh):
    placed = (
        P("user", None),
        P("user", BOTH),
        P("user", "leaf"),
        P(),
        P(BOTH, None),
        P(BOTH, None),
        P(),
        P(),
        P(),
        P(),
        P(None, "tensor"),
        P(None, None, "tensor"),
        P(None, "tensor"),
        P("tensor"),
    )
    return jax.shard_map(
        per_device,
        mesh=mesh,
        in_specs=placed,
        out_specs=(P("user", BOTH), P("user", None), P("user", "leaf")),
        check_vma=False,
    )
```

```python
import functools
import math

import jax
import jax.numpy as jnp
from jax import lax
from jax.experimental import pallas as pl
from jax.experimental.pallas import tpu as pltpu
from jax.sharding import PartitionSpec as P

SUB_NODES = 512
SUB_ITEMS = 512
BOTH = ("leaf", "tensor")
F32 = jnp.float32
BF16 = jnp.bfloat16


def small_lookup(table, index):
    hits = index[..., None] == jnp.arange(table.shape[0], dtype=jnp.int32)
    return jnp.sum(jnp.where(hits, table, 0), axis=-1)


def locate(ids, span, subtree_slot, rows):
    slot = small_lookup(subtree_slot, ids // span)
    per = rows // span
    return slot // per, slot % per * span + ids % span


def rank_in_row(marks):
    n = marks.shape[-1]
    at = jnp.arange(n, dtype=jnp.int32)
    before = (at[:, None] < at[None, :]).astype(BF16)
    return jnp.dot(marks.astype(BF16), before, preferred_element_type=F32).astype(jnp.int32)


def pick_rows(table, wanted):
    hot = (wanted[:, None] == jnp.arange(table.shape[0], dtype=jnp.int32)[None, :]).astype(BF16)
    return jnp.dot(hot, table, preferred_element_type=F32).astype(BF16)


def exchange_kernel(modes, sizes, *refs):
    n = len(modes)
    srcs, outs, send_sems, recv_sems = refs[:n], refs[n : 2 * n], refs[2 * n : 3 * n], refs[3 * n :]
    leaf, tensor, user = (lax.axis_index(axis) for axis in ("leaf", "tensor", "user"))
    leafs, tensors, users = sizes

    def group_of(mode):
        if mode in ("tensor", "user"):
            return mode
        return "wide"

    def extent(group):
        return {"wide": leafs * tensors, "tensor": tensors, "user": users}[group]

    def index(group):
        return {"wide": leaf * tensors + tensor, "tensor": tensor, "user": user}[group]

    def target(group, k):
        peer = (index(group) + k) % extent(group)
        if group == "wide":
            return peer, {"leaf": peer // tensors, "tensor": peer % tensors}
        return peer, {group: peer}

    def part(mode, src, peer, peer_leaf):
        if mode == "peer":
            return src.at[peer]
        if mode == "leaf":
            return src.at[peer_leaf]
        return src

    def copy(i, k):
        group = group_of(modes[i])
        peer, place = target(group, k)
        return pltpu.make_async_remote_copy(
            src_ref=part(modes[i], srcs[i], peer, place.get("leaf")),
            dst_ref=outs[i].at[index(group)],
            send_sem=send_sems[i].at[k - 1],
            recv_sem=recv_sems[i].at[k - 1],
            device_id=place,
            device_id_type=pl.DeviceIdType.MESH,
        )

    members = {}
    for i, mode in enumerate(modes):
        members.setdefault(group_of(mode), []).append(i)
    greeted = [g for g in members if not (g == "tensor" and "wide" in members)]

    barrier = pltpu.get_barrier_semaphore()
    for group in greeted:

        @pl.loop(1, extent(group))
        def _(k):
            pl.semaphore_signal(
                barrier,
                inc=1,
                device_id=target(group, k)[1],
                device_id_type=pl.DeviceIdType.MESH,
            )

    pl.semaphore_wait(barrier, sum(extent(group) - 1 for group in greeted))

    for group, held in members.items():

        @pl.loop(1, extent(group))
        def _(k):
            for i in held:
                copy(i, k).start()

    for mode, src, out in zip(modes, srcs, outs):
        at = index(group_of(mode))
        out[at] = part(mode, src, at, leaf)[...]

    for group, held in members.items():

        @pl.loop(1, extent(group))
        def _(k):
            for i in held:
                copy(i, k).wait()


def exchange(collective_id, *entries):
    sizes = tuple(lax.axis_size(axis) for axis in ("leaf", "tensor", "user"))
    modes = tuple(mode for mode, _ in entries)
    arrays = [array for _, array in entries]
    extents = [{"tensor": sizes[1], "user": sizes[2]}.get(m, sizes[0] * sizes[1]) for m in modes]
    outs = [
        jax.ShapeDtypeStruct(
            (size,) + (a.shape[1:] if mode in ("peer", "leaf") else a.shape), a.dtype
        )
        for mode, a, size in zip(modes, arrays, extents)
    ]
    return pl.pallas_call(
        functools.partial(exchange_kernel, modes, sizes),
        out_shape=outs,
        in_specs=[pl.BlockSpec(memory_space=pltpu.VMEM)] * len(arrays),
        out_specs=[pl.BlockSpec(memory_space=pltpu.VMEM)] * len(arrays),
        scratch_shapes=[pltpu.SemaphoreType.DMA((size - 1,)) for size in extents] * 2,
        compiler_params=pltpu.CompilerParams(
            collective_id=collective_id, has_side_effects=True, vmem_limit_bytes=32 << 20
        ),
    )(*arrays)


def rank_kernel_body(
    tensors, rows_ref, proj_ref, first_ref, own_proj, own_first, base0, base1, own0, own1,
    cross, bias, weight, out_ref,
):
    users, items, width = rows_ref.shape
    rows = rows_ref[...].reshape(users * items, width)
    cols = own_proj.shape[1]

    def dot(left, right):
        return jnp.dot(left, right, preferred_element_type=F32)

    def layer(proj, first, add0, add1):
        x0 = dot(rows, proj).reshape(users, items, cols) + add0
        return x0, x0 * (dot(rows, first).reshape(users, items, cols) + add1) + x0

    second = jnp.zeros((users * items, cols), F32)
    for t in range(tensors):
        proj = proj_ref[:, t].reshape(width, cols)
        first = first_ref[:, t].reshape(width, cols)
        _, x1 = layer(proj, first, base0[:, t : t + 1], base1[:, t : t + 1])
        x1 = x1.astype(BF16).reshape(users * items, cols)
        second += dot(x1, cross[t * cols : (t + 1) * cols, :])
    x0, x1 = layer(own_proj[...], own_first[...], own0[...], own1[...])
    x2 = x0 * (second.reshape(users, items, cols) + bias[...]) + x1
    out_ref[0] = jnp.sum(x2 * weight[...], axis=2)


def rank_rows(rows, proj_all, first_all, proj, first, base0, base1, own0, own1, cross, bias, weight):
    users, items, width = rows.shape
    tensors = proj_all.shape[1]
    cols = proj.shape[1]
    step = math.gcd(users, 4)
    full = pl.BlockSpec(proj_all.shape, lambda u: (0, 0, 0, 0))
    own = pl.BlockSpec((width, cols), lambda u: (0, 0))
    line = pl.BlockSpec((1, cols), lambda u: (0, 0))
    return pl.pallas_call(
        functools.partial(rank_kernel_body, tensors),
        grid=(users // step,),
        out_shape=jax.ShapeDtypeStruct((users // step, step, items), F32),
        in_specs=[
            pl.BlockSpec((step, items, width), lambda u: (u, 0, 0)),
            full, full, own, own,
            pl.BlockSpec((step, tensors, cols), lambda u: (u, 0, 0)),
            pl.BlockSpec((step, tensors, cols), lambda u: (u, 0, 0)),
            pl.BlockSpec((step, 1, cols), lambda u: (u, 0, 0)),
            pl.BlockSpec((step, 1, cols), lambda u: (u, 0, 0)),
            pl.BlockSpec(cross.shape, lambda u: (0, 0)),
            line, line,
        ],
        out_specs=pl.BlockSpec((1, step, items), lambda u: (u, 0, 0)),
        compiler_params=pltpu.CompilerParams(vmem_limit_bytes=48 << 20),
    )(rows, proj_all, first_all, proj, first, base0, base1, own0, own1, cross, bias, weight)


def request_lists(owner, coded, owners, cap):
    marks = owner[None, :] == jnp.arange(owners, dtype=jnp.int32)[:, None]
    rank = rank_in_row(marks)
    chosen = marks[:, None, :] & (
        rank[:, None, :] == jnp.arange(cap, dtype=jnp.int32)[None, :, None]
    )
    return chosen, jnp.sum(jnp.where(chosen, coded + 1, 0), axis=2) - 1


def per_device(
    user_feat,
    beam_nodes,
    item_ids,
    subtree_slot,
    node_table,
    item_table,
    mlp_user,
    mlp_node,
    mlp_bias,
    mlp_out,
    proj_in,
    cross_w,
    cross_b,
    out_w,
):
    leafs = lax.axis_size("leaf")
    tensors = lax.axis_size("tensor")
    owners = leafs * tensors
    tensor_at = lax.axis_index("tensor")
    users, beam = beam_nodes.shape
    items = item_ids.shape[1]
    width = user_feat.shape[1]
    two = 2 * width
    cols = proj_in.shape[1]

    user_count = lax.axis_size("user")
    share = width // user_count
    proj_here = proj_in[two:]
    proj_piece = lax.dynamic_slice(
        proj_here, (lax.axis_index("user") * share, 0), (share, cols)
    )

    requests = users * beam
    cap_b = max(2, -(-requests // owners))
    n_owner, n_local = locate(beam_nodes.reshape(-1), SUB_NODES, subtree_slot, node_table.shape[0])
    asker = jnp.arange(requests, dtype=jnp.int32) // beam
    n_chosen, n_list = request_lists(n_owner, n_local * users + asker, owners, cap_b)
    rows = users * items
    fetch = rows // tensors
    cap_i = max(2, -(-fetch // owners))
    i_owner, i_local = locate(item_ids.reshape(-1), SUB_ITEMS, subtree_slot, item_table.shape[0])
    i_owner, i_local = i_owner.reshape(tensors, fetch), i_local.reshape(tensors, fetch)
    run_owner = lax.dynamic_slice(i_owner, (tensor_at, 0), (1, fetch))[0]
    run_local = lax.dynamic_slice(i_local, (tensor_at, 0), (1, fetch))[0]
    _, i_list = request_lists(run_owner, run_local, owners, cap_i)
    lists = jnp.concatenate([n_list, i_list], axis=1)
    lanes = -(-lists.shape[1] // 128) * 128
    lists = jnp.pad(lists, ((0, 0), (0, lanes - lists.shape[1])))[:, None, :]
    asked, proj_wide = exchange(0, ("peer", lists), ("tensor", proj_piece))
    first_piece = jnp.dot(
        jnp.moveaxis(proj_wide, 0, 1).reshape(share, tensors * cols),
        cross_w[0],
        preferred_element_type=F32,
    ).astype(BF16)
    n_asked = asked[:, 0, :cap_b].reshape(-1)
    i_asked = asked[:, 0, cap_b : cap_b + cap_i].reshape(-1)

    sent = pick_rows(item_table, i_asked).reshape(leafs, tensors * cap_i, width)
    held = n_asked >= 0
    node_rows = pick_rows(node_table, jnp.where(held, n_asked // users, -1))
    user_hot = (n_asked % users)[:, None] == jnp.arange(users, dtype=jnp.int32)[None, :]
    user_rows = jnp.dot(user_hot.astype(BF16), user_feat, preferred_element_type=F32).astype(BF16)
    pre = (
        jnp.dot(user_rows, mlp_user, preferred_element_type=F32)
        + jnp.dot(node_rows, mlp_node, preferred_element_type=F32)
        + mlp_bias
    )
    hidden = jax.nn.silu(pre).astype(BF16)
    scores = jnp.dot(hidden, mlp_out, preferred_element_type=F32)
    gate = jnp.where(user_hot & held[:, None], jax.nn.sigmoid(scores)[:, None], 0.0)
    numerator = lax.dot_general(
        gate, node_rows.astype(F32), (((0,), (0,)), ((), ())), precision=lax.Precision.HIGHEST
    )
    back_lanes = -(-cap_b // 128) * 128
    back = jnp.pad(scores.reshape(owners, cap_b), ((0, 0), (0, back_lanes - cap_b)))[:, None, :]
    sums, scored, first_wide, proj_all, arrived = exchange(
        1,
        ("all", numerator),
        ("peer", back),
        ("tensor", first_piece),
        ("user", proj_wide),
        ("leaf", sent),
    )
    interest = jnp.sum(sums, axis=0) / math.sqrt(owners * beam)
    own_scores = scored[:, 0, :cap_b]
    beam_score = jnp.sum(
        jnp.where(n_chosen, own_scores[:, :, None], 0.0), axis=(0, 1)
    ).reshape(users, beam)

    shared = jnp.concatenate([user_feat, interest.astype(BF16)], axis=1)
    own0 = jnp.dot(shared, proj_in[:two], preferred_element_type=F32)
    all0, first_all = exchange(2, ("tensor", own0), ("user", first_wide))
    base0 = jnp.moveaxis(all0, 0, 1)
    flat0 = base0.reshape(users, tensors * cols).astype(BF16)
    own1 = jnp.dot(flat0, cross_w[0], preferred_element_type=F32) + cross_b[0]
    (all1,) = exchange(3, ("tensor", own1))
    base1 = jnp.moveaxis(all1, 0, 1)

    run_marks = i_owner[:, None, :] == jnp.arange(owners, dtype=jnp.int32)[None, :, None]
    run_rank = jnp.sum(jnp.where(run_marks, rank_in_row(run_marks), 0), axis=1)
    place = run_rank + i_owner * cap_i
    by_run = jnp.moveaxis(arrived.reshape(owners, tensors, cap_i, width), 1, 0)
    hot = (place[:, :, None] == jnp.arange(owners * cap_i, dtype=jnp.int32)).astype(BF16)
    item_rows = jnp.einsum(
        "tfs,tsd->tfd", hot, by_run.reshape(tensors, owners * cap_i, width),
        preferred_element_type=F32,
    ).astype(BF16).reshape(users, items, width)

    first_here = lax.dynamic_slice(
        first_all, (0, tensor_at, 0, 0), (user_count, 1, share, cols)
    ).reshape(width, cols)
    partial = rank_rows(
        item_rows, proj_all, first_all, proj_here, first_here, base0, base1,
        own0[:, None, :], own1[:, None, :], cross_w[1], cross_b[1][None, :],
        out_w.astype(F32)[None, :],
    )
    (parts,) = exchange(4, ("tensor", partial.reshape(users, items)))
    logit = jnp.sum(parts, axis=0)
    return (beam_score, interest, logit)


def solution(mesh):
    placed = (
        P("user", None),
        P("user", BOTH),
        P("user", "leaf"),
        P(),
        P(BOTH, None),
        P(BOTH, None),
        P(),
        P(),
        P(),
        P(),
        P(None, "tensor"),
        P(None, None, "tensor"),
        P(None, "tensor"),
        P("tensor"),
    )
    return jax.shard_map(
        per_device,
        mesh=mesh,
        in_specs=placed,
        out_specs=(P("user", BOTH), P("user", None), P("user", "leaf")),
        check_vma=False,
    )
```

```python
import functools
import math

import jax
import jax.numpy as jnp
from jax import lax
from jax.experimental import pallas as pl
from jax.experimental.pallas import tpu as pltpu
from jax.sharding import PartitionSpec as P

SUB_NODES = 512
SUB_ITEMS = 512
BOTH = ("leaf", "tensor")
F32 = jnp.float32
BF16 = jnp.bfloat16


def small_lookup(table, index):
    hits = index[..., None] == jnp.arange(table.shape[0], dtype=jnp.int32)
    return jnp.sum(jnp.where(hits, table, 0), axis=-1)


def locate(ids, span, subtree_slot, rows):
    slot = small_lookup(subtree_slot, ids // span)
    per = rows // span
    return slot // per, slot % per * span + ids % span


def rank_in_row(marks):
    n = marks.shape[-1]
    at = jnp.arange(n, dtype=jnp.int32)
    before = (at[:, None] < at[None, :]).astype(BF16)
    return jnp.dot(marks.astype(BF16), before, preferred_element_type=F32).astype(jnp.int32)


def pick_rows(table, wanted):
    hot = (wanted[:, None] == jnp.arange(table.shape[0], dtype=jnp.int32)[None, :]).astype(BF16)
    return jnp.dot(hot, table, preferred_element_type=F32).astype(BF16)


def exchange_kernel(modes, sizes, *refs):
    n = len(modes)
    srcs, outs, send_sems, recv_sems = refs[:n], refs[n : 2 * n], refs[2 * n : 3 * n], refs[3 * n :]
    leaf, tensor, user = (lax.axis_index(axis) for axis in ("leaf", "tensor", "user"))
    leafs, tensors, users = sizes

    def group_of(mode):
        if mode in ("tensor", "user"):
            return mode
        return "wide"

    def extent(group):
        return {"wide": leafs * tensors, "tensor": tensors, "user": users}[group]

    def index(group):
        return {"wide": leaf * tensors + tensor, "tensor": tensor, "user": user}[group]

    def target(group, k):
        peer = (index(group) + k) % extent(group)
        if group == "wide":
            return peer, {"leaf": peer // tensors, "tensor": peer % tensors}
        return peer, {group: peer}

    def part(mode, src, peer, peer_leaf):
        if mode == "peer":
            return src.at[peer]
        if mode == "leaf":
            return src.at[peer_leaf]
        return src

    def copy(i, k):
        group = group_of(modes[i])
        peer, place = target(group, k)
        return pltpu.make_async_remote_copy(
            src_ref=part(modes[i], srcs[i], peer, place.get("leaf")),
            dst_ref=outs[i].at[index(group)],
            send_sem=send_sems[i].at[k - 1],
            recv_sem=recv_sems[i].at[k - 1],
            device_id=place,
            device_id_type=pl.DeviceIdType.MESH,
        )

    members = {}
    for i, mode in enumerate(modes):
        members.setdefault(group_of(mode), []).append(i)
    greeted = [g for g in members if not (g == "tensor" and "wide" in members)]

    barrier = pltpu.get_barrier_semaphore()
    for group in greeted:

        @pl.loop(1, extent(group))
        def _(k):
            pl.semaphore_signal(
                barrier,
                inc=1,
                device_id=target(group, k)[1],
                device_id_type=pl.DeviceIdType.MESH,
            )

    pl.semaphore_wait(barrier, sum(extent(group) - 1 for group in greeted))

    for group, held in members.items():

        @pl.loop(1, extent(group))
        def _(k):
            for i in held:
                copy(i, k).start()

    for mode, src, out in zip(modes, srcs, outs):
        at = index(group_of(mode))
        out[at] = part(mode, src, at, leaf)[...]

    for group, held in members.items():

        @pl.loop(1, extent(group))
        def _(k):
            for i in held:
                copy(i, k).wait()


def exchange(collective_id, *entries):
    sizes = tuple(lax.axis_size(axis) for axis in ("leaf", "tensor", "user"))
    modes = tuple(mode for mode, _ in entries)
    arrays = [array for _, array in entries]
    extents = [{"tensor": sizes[1], "user": sizes[2]}.get(m, sizes[0] * sizes[1]) for m in modes]
    outs = [
        jax.ShapeDtypeStruct(
            (size,) + (a.shape[1:] if mode in ("peer", "leaf") else a.shape), a.dtype
        )
        for mode, a, size in zip(modes, arrays, extents)
    ]
    return pl.pallas_call(
        functools.partial(exchange_kernel, modes, sizes),
        out_shape=outs,
        in_specs=[pl.BlockSpec(memory_space=pltpu.VMEM)] * len(arrays),
        out_specs=[pl.BlockSpec(memory_space=pltpu.VMEM)] * len(arrays),
        scratch_shapes=[pltpu.SemaphoreType.DMA((size - 1,)) for size in extents] * 2,
        compiler_params=pltpu.CompilerParams(
            collective_id=collective_id, has_side_effects=True, vmem_limit_bytes=32 << 20
        ),
    )(*arrays)


def rank_kernel_body(
    sizes, rows_ref, proj_ref, first_wide, own_proj, own0, cross, bias, weight, out_ref,
    first_ref, all0, all1, own1, part, parts,
    first_send, first_recv, send0, recv0, send1, recv1, send2, recv2,
):
    tensors, user_count = sizes
    tensor, user = lax.axis_index("tensor"), lax.axis_index("user")
    users, items, width = rows_ref.shape
    cols = own_proj.shape[1]
    extent = {"tensor": tensors, "user": user_count}
    index = {"tensor": tensor, "user": user}

    def each(axis, body):
        pl.loop(1, extent[axis])(body)

    def target(axis, k):
        return {axis: (index[axis] + k) % extent[axis]}

    def copy(axis, src, out, sends, recvs, k):
        return pltpu.make_async_remote_copy(
            src_ref=src,
            dst_ref=out.at[index[axis]],
            send_sem=sends.at[k - 1],
            recv_sem=recvs.at[k - 1],
            device_id=target(axis, k),
            device_id_type=pl.DeviceIdType.MESH,
        )

    def begin(*what):
        each(what[0], lambda k: copy(*what, k).start())
        what[2][index[what[0]]] = what[1][...]

    def finish(*what):
        each(what[0], lambda k: copy(*what, k).wait())

    def dot(left, right):
        return jnp.dot(left, right, preferred_element_type=F32)

    barrier = pltpu.get_barrier_semaphore()
    for axis in extent:
        each(
            axis,
            lambda k: pl.semaphore_signal(
                barrier, inc=1, device_id=target(axis, k), device_id_type=pl.DeviceIdType.MESH
            ),
        )
    pl.semaphore_wait(barrier, tensors + user_count - 2)

    shares = ("tensor", own0, all0, send0, recv0)
    products = ("tensor", own1, all1, send1, recv1)
    weights = ("user", first_wide, first_ref, first_send, first_recv)
    logits = ("tensor", part, parts, send2, recv2)
    begin(*shares)
    begin(*weights)
    finish(*shares)
    total = bias[0:1]
    for t in range(tensors):
        total = total + dot(all0[t].astype(BF16), cross[0, t * cols : (t + 1) * cols, :])
    own1[...] = total
    begin(*products)
    finish(*weights)
    finish(*products)

    def layer(rows, proj, first, add0, add1):
        count = add0.shape[0]
        x0 = dot(rows, proj).reshape(count, items, cols) + add0[:, None, :]
        return x0, x0 * (dot(rows, first).reshape(count, items, cols) + add1[:, None, :]) + x0

    step = math.gcd(users, 4)
    for u in range(0, users, step):
        held = slice(u, u + step)
        rows = rows_ref[held].reshape(step * items, width)
        second = jnp.zeros((step * items, cols), F32)
        for t in range(tensors):
            proj = proj_ref[:, t].reshape(width, cols)
            first = first_ref[:, t].reshape(width, cols)
            _, x1 = layer(rows, proj, first, all0[t, held], all1[t, held])
            x1 = x1.astype(BF16).reshape(step * items, cols)
            second += dot(x1, cross[1, t * cols : (t + 1) * cols, :])
        own_first = first_ref[:, tensor].reshape(width, cols)
        x0, x1 = layer(rows, own_proj[...], own_first, own0[held], own1[held])
        x2 = x0 * (second.reshape(step, items, cols) + bias[1:2]) + x1
        part[held] = jnp.sum(x2 * weight[...], axis=2)
    begin(*logits)
    finish(*logits)
    out_ref[...] = jnp.sum(parts[...], axis=0)


def rank_rows(collective_id, rows, proj_all, first_wide, own_proj, own0, cross, bias, weight):
    users, items, width = rows.shape
    user_count, tensors = proj_all.shape[:2]
    cols = own_proj.shape[1]
    vmem = pl.BlockSpec(memory_space=pltpu.VMEM)
    return pl.pallas_call(
        functools.partial(rank_kernel_body, (tensors, user_count)),
        out_shape=jax.ShapeDtypeStruct((users, items), F32),
        in_specs=[vmem] * 8,
        out_specs=vmem,
        scratch_shapes=[
            pltpu.VMEM(proj_all.shape, BF16),
            pltpu.VMEM((tensors, users, cols), F32),
            pltpu.VMEM((tensors, users, cols), F32),
            pltpu.VMEM((users, cols), F32),
            pltpu.VMEM((users, items), F32),
            pltpu.VMEM((tensors, users, items), F32),
        ]
        + [pltpu.SemaphoreType.DMA((user_count - 1,))] * 2
        + [pltpu.SemaphoreType.DMA((tensors - 1,))] * 6,
        compiler_params=pltpu.CompilerParams(
            collective_id=collective_id, has_side_effects=True, vmem_limit_bytes=48 << 20
        ),
    )(rows, proj_all, first_wide, own_proj, own0, cross, bias, weight)


def request_lists(owner, coded, owners, cap):
    marks = owner[None, :] == jnp.arange(owners, dtype=jnp.int32)[:, None]
    rank = rank_in_row(marks)
    chosen = marks[:, None, :] & (
        rank[:, None, :] == jnp.arange(cap, dtype=jnp.int32)[None, :, None]
    )
    return chosen, jnp.sum(jnp.where(chosen, coded + 1, 0), axis=2) - 1


def per_device(
    user_feat,
    beam_nodes,
    item_ids,
    subtree_slot,
    node_table,
    item_table,
    mlp_user,
    mlp_node,
    mlp_bias,
    mlp_out,
    proj_in,
    cross_w,
    cross_b,
    out_w,
):
    leafs = lax.axis_size("leaf")
    tensors = lax.axis_size("tensor")
    owners = leafs * tensors
    tensor_at = lax.axis_index("tensor")
    users, beam = beam_nodes.shape
    items = item_ids.shape[1]
    width = user_feat.shape[1]
    two = 2 * width
    cols = proj_in.shape[1]

    user_count = lax.axis_size("user")
    share = width // user_count
    proj_here = proj_in[two:]
    proj_piece = lax.dynamic_slice(
        proj_here, (lax.axis_index("user") * share, 0), (share, cols)
    )

    requests = users * beam
    cap_b = max(2, -(-requests // owners))
    n_owner, n_local = locate(beam_nodes.reshape(-1), SUB_NODES, subtree_slot, node_table.shape[0])
    asker = jnp.arange(requests, dtype=jnp.int32) // beam
    n_chosen, n_list = request_lists(n_owner, n_local * users + asker, owners, cap_b)
    rows = users * items
    fetch = rows // tensors
    cap_i = max(2, -(-fetch // owners))
    i_owner, i_local = locate(item_ids.reshape(-1), SUB_ITEMS, subtree_slot, item_table.shape[0])
    i_owner, i_local = i_owner.reshape(tensors, fetch), i_local.reshape(tensors, fetch)
    run_owner = lax.dynamic_slice(i_owner, (tensor_at, 0), (1, fetch))[0]
    run_local = lax.dynamic_slice(i_local, (tensor_at, 0), (1, fetch))[0]
    _, i_list = request_lists(run_owner, run_local, owners, cap_i)
    lists = jnp.concatenate([n_list, i_list], axis=1)
    lanes = -(-lists.shape[1] // 128) * 128
    lists = jnp.pad(lists, ((0, 0), (0, lanes - lists.shape[1])))[:, None, :]
    asked, proj_wide = exchange(0, ("peer", lists), ("tensor", proj_piece))
    first_piece = jnp.dot(
        jnp.moveaxis(proj_wide, 0, 1).reshape(share, tensors * cols),
        cross_w[0],
        preferred_element_type=F32,
    ).astype(BF16)
    n_asked = asked[:, 0, :cap_b].reshape(-1)
    i_asked = asked[:, 0, cap_b : cap_b + cap_i].reshape(-1)

    sent = pick_rows(item_table, i_asked).reshape(leafs, tensors * cap_i, width)
    held = n_asked >= 0
    node_rows = pick_rows(node_table, jnp.where(held, n_asked // users, -1))
    user_hot = (n_asked % users)[:, None] == jnp.arange(users, dtype=jnp.int32)[None, :]
    user_rows = jnp.dot(user_hot.astype(BF16), user_feat, preferred_element_type=F32).astype(BF16)
    pre = (
        jnp.dot(user_rows, mlp_user, preferred_element_type=F32)
        + jnp.dot(node_rows, mlp_node, preferred_element_type=F32)
        + mlp_bias
    )
    hidden = jax.nn.silu(pre).astype(BF16)
    scores = jnp.dot(hidden, mlp_out, preferred_element_type=F32)
    gate = jnp.where(user_hot & held[:, None], jax.nn.sigmoid(scores)[:, None], 0.0)
    numerator = lax.dot_general(
        gate, node_rows.astype(F32), (((0,), (0,)), ((), ())), precision=lax.Precision.HIGHEST
    )
    back_lanes = -(-cap_b // 128) * 128
    back = jnp.pad(scores.reshape(owners, cap_b), ((0, 0), (0, back_lanes - cap_b)))[:, None, :]
    sums, scored, first_wide, proj_all, arrived = exchange(
        1,
        ("all", numerator),
        ("peer", back),
        ("tensor", first_piece),
        ("user", proj_wide),
        ("leaf", sent),
    )
    interest = jnp.sum(sums, axis=0) / math.sqrt(owners * beam)
    own_scores = scored[:, 0, :cap_b]
    beam_score = jnp.sum(
        jnp.where(n_chosen, own_scores[:, :, None], 0.0), axis=(0, 1)
    ).reshape(users, beam)

    shared = jnp.concatenate([user_feat, interest.astype(BF16)], axis=1)
    own0 = jnp.dot(shared, proj_in[:two], preferred_element_type=F32)
    run_marks = i_owner[:, None, :] == jnp.arange(owners, dtype=jnp.int32)[None, :, None]
    run_rank = jnp.sum(jnp.where(run_marks, rank_in_row(run_marks), 0), axis=1)
    place = run_rank + i_owner * cap_i
    by_run = jnp.moveaxis(arrived.reshape(owners, tensors, cap_i, width), 1, 0)
    hot = (place[:, :, None] == jnp.arange(owners * cap_i, dtype=jnp.int32)).astype(BF16)
    item_rows = jnp.einsum(
        "tfs,tsd->tfd", hot, by_run.reshape(tensors, owners * cap_i, width),
        preferred_element_type=F32,
    ).astype(BF16).reshape(users, items, width)

    logit = rank_rows(
        2, item_rows, proj_all, first_wide, proj_here, own0, cross_w, cross_b,
        out_w.astype(F32)[None, :],
    )
    return (beam_score, interest, logit)


def solution(mesh):
    placed = (
        P("user", None),
        P("user", BOTH),
        P("user", "leaf"),
        P(),
        P(BOTH, None),
        P(BOTH, None),
        P(),
        P(),
        P(),
        P(),
        P(None, "tensor"),
        P(None, None, "tensor"),
        P(None, "tensor"),
        P("tensor"),
    )
    return jax.shard_map(
        per_device,
        mesh=mesh,
        in_specs=placed,
        out_specs=(P("user", BOTH), P("user", None), P("user", "leaf")),
        check_vma=False,
    )
```
